256 devices in a mesh: grp: 8 (over y_hi, x), aux: 32 (over y_lo, z, core).
Axes of the slice: x: 4, y: 4 (y_hi: 2, y_lo: 2; y = y_hi * 2 + y_lo), z: 8, core: 2. Of those that a mesh axis runs over, the one named last changes fastest.
Arguments:
- integrals: bfloat16 [2048, 256, 512], P('aux', 'grp'), may hold values from -0.75 to 0.75
- metric: bfloat16 [2048, 2048], replicated, may hold values from -0.125 to 0.125
- occupied_energy: float32 [256], replicated, may hold values from -2 to -0.5
- virtual_energy: float32 [512], replicated, may hold values from 0.2 to 3
- plan: int32 [4, 32], replicated, may hold values from 0 to 7
Outputs:
- density: bfloat16 [2048, 256, 512], P('aux', 'grp')
The draws below stay inside these ranges and needn't reach their ends.
All inputs are finite; a program needn't handle non-finite values.
Results may differ from the reference program's by a relative error of at most 0.0053.
Values may be sent and summed in bfloat16 or wider, within the bound.
No kernel may reach another device: no remote copies, remote signals or barrier semaphores. Data moves between devices by JAX's collectives and lax.ppermute only.
A program may use at most 128 MiB of HBM per device.

```python
import math
import jax
import jax.numpy as jnp
from jax import lax

NVIRT = 512
NAUX = 2048
OCC_DEV = 1
STEPS = 4
OCC_GRP = 32
NOCC = 256
N_GRP = 8
N_AUX = 32


def with_ends(result, own_key, low, high):
    longest = result.shape.index(max(result.shape))
    spots = []
    for shift in (0, 1):
        where = [jax.random.randint(jax.random.fold_in(own_key, axis), (), 0, length) for axis, length in enumerate(result.shape)]
        where[longest] = (where[longest] + shift) % result.shape[longest]
        spots.append(tuple(where))
    return result.at[spots[0]].set(low).at[spots[1]].set(high)


def steps_of(stream_key, shape, split, least, high):
    gain = 1.0
    for dim, blocks in split:
        draws = jax.random.uniform(jax.random.fold_in(jax.random.fold_in(stream_key, 6), dim), (blocks,), jnp.float32, least / len(split), high / len(split))
        gain = gain * jnp.repeat(jnp.exp(draws), shape[dim] // blocks).reshape((-1,) + (1,) * (len(shape) - 1 - dim))
    return gain


def centred(own_key, shape, width, bound, pieces=(), held_as=jnp.bfloat16):
    entries = width * jax.random.normal(own_key, shape, jnp.float32)
    if pieces:
        entries = entries * steps_of(own_key, shape, pieces, -0.22, 0.18)
    return jnp.clip(entries, -bound, bound).astype(held_as)


def setup_inputs(seed: int = 0) -> dict:
    seeds = jax.random.split(jax.random.key(seed), 6)
    return {
        "integrals": centred(seeds[0], (NAUX, NOCC, NVIRT), 0.12, 0.75, ((0, 32), (1, 8))),
        "metric": centred(seeds[1], (NAUX, NAUX), NAUX ** -0.5, 0.125),
        "occupied_energy": jnp.clip(jax.random.uniform(seeds[2], (NOCC,), jnp.float32, -2.0, -0.5), -2.0, -0.5),
        "virtual_energy": jnp.clip(jnp.exp(jax.random.uniform(seeds[3], (NVIRT,), jnp.float32, math.log(0.2), math.log(3.0))), 0.2, 3.0),
        "plan": with_ends(jax.random.randint(seeds[4], (STEPS, N_AUX), 0, N_GRP), jax.random.fold_in(seeds[4], 1), 0, N_GRP - 1).astype(jnp.int32),
    }


def pair_term(own_block, partner, own_energy, partner_energy, virtual_energy):
    coulomb = jnp.einsum('qia,qjb->ijab', own_block.astype(jnp.float32), partner.astype(jnp.float32))
    denominator = (own_energy[:, None, None, None] + partner_energy[None, :, None, None]
                   - virtual_energy[None, None, :, None] - virtual_energy[None, None, None, :])
    amplitude = ((2.0 * coulomb - jnp.swapaxes(coulomb, 2, 3)) / denominator).astype(jnp.bfloat16)
    return jnp.einsum('ijab,qjb->qia', amplitude.astype(jnp.float32), partner.astype(jnp.float32))


def reference(integrals, metric, occupied_energy, virtual_energy, plan):
    metric_wide = metric.astype(jnp.float32)

    def transform(group_index):
        slab_rows = lax.dynamic_slice_in_dim(integrals, group_index * OCC_GRP, OCC_GRP, 1)
        product = jnp.dot(metric_wide, slab_rows.reshape(NAUX, OCC_GRP * NVIRT).astype(jnp.float32))
        product = product.astype(jnp.bfloat16).reshape(NAUX, N_AUX, OCC_DEV, NVIRT)
        return jnp.moveaxis(product, 1, 0)

    coeff = lax.map(transform, jnp.arange(N_GRP, dtype=jnp.int32))
    coeff = coeff.reshape(N_GRP * N_AUX, NAUX, OCC_DEV, NVIRT)

    def pair_block(block_index):
        own_block = lax.dynamic_index_in_dim(coeff, block_index, 0, keepdims=False)
        aux_place = (block_index % N_AUX).astype(jnp.int32)
        own_energy = lax.dynamic_slice_in_dim(occupied_energy, block_index * OCC_DEV, OCC_DEV)
        density_sum = jnp.zeros((NAUX, OCC_DEV, NVIRT), jnp.float32)
        for step_index in range(STEPS):
            owner_group = lax.dynamic_index_in_dim(plan[step_index], aux_place, 0, keepdims=False)
            partner_index = (owner_group * N_AUX + aux_place).astype(jnp.int32)
            partner = lax.dynamic_index_in_dim(coeff, partner_index, 0, keepdims=False)
            partner_energy = lax.dynamic_slice_in_dim(occupied_energy, partner_index * OCC_DEV, OCC_DEV)
            density_sum = density_sum + pair_term(own_block, partner, own_energy, partner_energy, virtual_energy)
        return density_sum.astype(jnp.bfloat16)

    density = lax.map(pair_block, jnp.arange(N_GRP * N_AUX, dtype=jnp.int32))
    return jnp.moveaxis(density, 0, 1).reshape(NAUX, NOCC, NVIRT)
```

```python
import jax
import jax.numpy as jnp
from jax import lax
from jax.experimental import pallas as pl
from jax.experimental.pallas import tpu as pltpu
from jax.sharding import Mesh
from jax.sharding import PartitionSpec as P

SPLIT = (("yh", 2), ("x", 4), ("yl", 2), ("z", 8), ("c", 2))
AUX = ("yl", "z", "c")
PLACE = ("c", "x")
CHUNKS = 2


def pair_kernel(energy_ref, own0, own1, part0, part1, row_ref, col_ref, out_ref, own_t, total):
    s = pl.program_id(0)
    half = own0.shape[1]

    @pl.when(s == 0)
    def _():
        own_t[:half, :] = own0[...].T
        own_t[half:, :] = own1[...].T

    partner = jnp.concatenate(
        [part0[...].reshape(own0.shape), part1[...].reshape(own0.shape)], axis=1
    )
    coulomb = jnp.dot(own_t[...], partner, preferred_element_type=jnp.float32)
    shift = energy_ref[4] + energy_ref[s]
    denominator = shift - row_ref[...] - col_ref[...]
    amplitude = ((2.0 * coulomb - coulomb.T) / denominator).astype(jnp.bfloat16)
    term = lax.dot_general(
        partner, amplitude, (((1,), (1,)), ((), ())), preferred_element_type=jnp.float32
    )

    @pl.when(s == 0)
    def _():
        total[...] = term

    @pl.when(s > 0)
    def _():
        total[...] += term

    @pl.when(s == pl.num_programs(0) - 1)
    def _():
        out_ref[...] = total[...].astype(out_ref.dtype)


def pair_terms(energies, owns, parts, virtual_energy):
    rows, half = owns[0].shape
    virt = 2 * half
    steps = parts[0].shape[1]
    whole = pl.BlockSpec((rows, half), lambda s: (0, 0))
    part = pl.BlockSpec((8, 1, rows // 8, half), lambda s: (0, s, 0, 0))
    smem = pl.BlockSpec(memory_space=pltpu.SMEM)
    return pl.pallas_call(
        pair_kernel,
        out_shape=jax.ShapeDtypeStruct((rows, virt), jnp.bfloat16),
        grid=(steps,),
        in_specs=[
            smem,
            whole,
            whole,
            part,
            part,
            pl.BlockSpec((virt, 1), lambda s: (0, 0)),
            pl.BlockSpec((1, virt), lambda s: (0, 0)),
        ],
        out_specs=pl.BlockSpec((rows, virt), lambda s: (0, 0)),
        scratch_shapes=[
            pltpu.VMEM((virt, rows), jnp.bfloat16),
            pltpu.VMEM((rows, virt), jnp.float32),
        ],
        compiler_params=pltpu.CompilerParams(vmem_limit_bytes=44 * 2**20),
        cost_estimate=pl.CostEstimate(
            flops=steps * 4 * rows * virt * virt,
            bytes_accessed=(steps + 2) * rows * virt * 2,
            transcendentals=0,
        ),
        name="pair_terms",
    )(energies, *owns, *parts, virtual_energy[:, None], virtual_energy[None, :])


def body(integrals, metric, occupied_energy, virtual_energy, plan):
    aux_rows = metric.shape[0]
    shard, _, virt = integrals.shape
    width = virt // CHUNKS
    y, x, yl, z, c = (lax.axis_index(name) for name, _ in SPLIT)
    place = (yl * 8 + z) * 2 + y
    wanted = lax.dynamic_index_in_dim(plan, place, 1, keepdims=False)
    own_energy = lax.dynamic_slice_in_dim(occupied_energy, (c * 4 + x) * 32 + place, 1)
    partner_energy = occupied_energy[wanted * 32 + place]
    energies = jnp.concatenate([partner_energy, own_energy])
    sent = integrals.reshape(shard, 16, 2, CHUNKS, width).transpose(3, 2, 1, 0, 4)
    owns, parts = [], []
    for k in range(CHUNKS):
        turned = lax.all_to_all(sent[k], "yh", 0, 0, tiled=True)
        turned = turned.transpose(1, 0, 2, 3).reshape(32, shard, width)
        received = lax.all_to_all(turned, AUX, 0, 0, tiled=True).reshape(aux_rows, width)
        own = jnp.dot(metric, received, preferred_element_type=jnp.float32).astype(jnp.bfloat16)
        owns.append(own)
        slices = lax.all_to_all(
            own.reshape(8, aux_rows // 8, width), PLACE, 0, 0, tiled=True
        )
        picked = jnp.stack(
            [
                lax.dynamic_index_in_dim(slices, wanted[s], 0, keepdims=False)
                for s in range(plan.shape[0])
            ]
        )
        along = lax.all_to_all(jnp.broadcast_to(picked, (4, *picked.shape)), "x", 0, 0, tiled=True)
        along = along.reshape(4, *picked.shape)
        both = lax.all_to_all(jnp.broadcast_to(along, (2, *along.shape)), "c", 0, 0, tiled=True)
        parts.append(both.reshape(8, *picked.shape))
    density = pair_terms(energies, owns, parts, virtual_energy)
    density = density.reshape(32, 2, shard // 2, virt)
    outs = []
    for k in range(2):
        gone = lax.all_to_all(density[:, k], AUX, 0, 0, tiled=True)
        gone = gone.reshape(16, 2, shard // 2, virt).transpose(1, 0, 2, 3)
        back = lax.all_to_all(gone, "yh", 0, 0, tiled=True)
        outs.append(back.transpose(2, 1, 0, 3).reshape(shard // 2, 32, virt))
    return jnp.concatenate(outs)


def solution(mesh):
    names = tuple(name for name, _ in SPLIT)
    split = Mesh(mesh.devices.reshape(*(size for _, size in SPLIT)), names)
    placed = P(AUX, ("yh", "x"), None)
    return jax.shard_map(
        body, mesh=split, in_specs=(placed, P(), P(), P(), P()), out_specs=placed, check_vma=False
    )
```

```python
import jax
import jax.numpy as jnp
from jax import lax
from jax.experimental import pallas as pl
from jax.experimental.pallas import tpu as pltpu
from jax.sharding import Mesh
from jax.sharding import PartitionSpec as P

SPLIT = (("yh", 2), ("x", 4), ("yl", 2), ("z", 8), ("c", 2))
AUX = ("yl", "z", "c")
TURNED = ("c", "yl", "z")
CHUNKS = 2
SMEM = pl.BlockSpec(memory_space=pltpu.SMEM)
VMEM = pl.BlockSpec(memory_space=pltpu.VMEM)


def shifted(array, axis, by):
    size = lax.axis_size(axis)
    return lax.ppermute(array, axis, [(i, (i + by) % size) for i in range(size)])


def slice_of(spot, turn, step):
    return (spot[1] ^ turn) * 4 + (spot[0] + step) % 4


def transform_kernel(spot, metric_ref, received_ref, *rest):
    outs, ordered = rest[:4], rest[4]
    r = pl.program_id(0)
    rows, width = ordered.shape

    @pl.when(r == 0)
    def _():
        for turn in range(2):
            for q in range(16):
                at = (q * 2 + turn) * 64
                ordered[at : at + 64, :] = received_ref[turn * 16 + q]

    value = jnp.dot(metric_ref[...], ordered[...], preferred_element_type=jnp.float32)
    value = value.astype(jnp.bfloat16)
    for step in range(4):
        for turn in range(2):

            @pl.when(r == turn * 4 + step)
            def _():
                outs[step][turn] = value


def transform(spot, metric, received):
    rows = metric.shape[0]
    width = received.shape[2]
    piece = jax.ShapeDtypeStruct((2, rows // 8, width), jnp.bfloat16)
    return pl.pallas_call(
        transform_kernel,
        out_shape=[piece] * 4,
        grid_spec=pltpu.PrefetchScalarGridSpec(
            num_scalar_prefetch=1,
            grid=(8,),
            in_specs=[
                pl.BlockSpec((rows // 8, rows), lambda r, spot: (slice_of(spot, r // 4, r % 4), 0)),
                pl.BlockSpec(received.shape, lambda r, spot: (0, 0, 0)),
            ],
            out_specs=[pl.BlockSpec(piece.shape, lambda r, spot: (0, 0, 0))] * 4,
            scratch_shapes=[pltpu.VMEM((rows, width), jnp.bfloat16)],
        ),
        compiler_params=pltpu.CompilerParams(vmem_limit_bytes=16 * 2**20),
        cost_estimate=pl.CostEstimate(
            flops=2 * rows * rows * width, bytes_accessed=2 * rows * (rows + 2 * width), transcendentals=0
        ),
        name="transform",
    )(spot, metric, received)


def pick_kernel(spot, plan, *refs):
    pieces, keep, give = refs[:4], refs[4], refs[5]
    for s in range(keep.shape[0]):
        step = (spot[0] - plan[s, spot[2]] % 4) % 4
        for d in range(4):

            @pl.when(step == d)
            def _():
                keep[s] = pieces[d][0]
                give[s] = pieces[d][1]


def pick(spot, plan, pieces):
    out = jax.ShapeDtypeStruct((plan.shape[0], *pieces[0].shape[1:]), jnp.bfloat16)
    return pl.pallas_call(
        pick_kernel,
        out_shape=[out, out],
        in_specs=[SMEM, SMEM] + [VMEM] * 4,
        out_specs=[VMEM, VMEM],
        compiler_params=pltpu.CompilerParams(vmem_limit_bytes=12 * 2**20),
        cost_estimate=pl.CostEstimate(flops=0, bytes_accessed=2 * 2**20, transcendentals=0),
        name="pick",
    )(spot, plan, *pieces)


def choose_kernel(spot, plan, keep, given, out):
    for s in range(keep.shape[0]):
        same = plan[s, spot[2]] // 4 == spot[1]

        @pl.when(same)
        def _():
            out[s] = keep[s]

        @pl.when(jnp.logical_not(same))
        def _():
            out[s] = given[s]


def choose(spot, plan, keep, given):
    return pl.pallas_call(
        choose_kernel,
        out_shape=jax.ShapeDtypeStruct(keep.shape, keep.dtype),
        in_specs=[SMEM, SMEM, VMEM, VMEM],
        out_specs=VMEM,
        compiler_params=pltpu.CompilerParams(vmem_limit_bytes=8 * 2**20),
        cost_estimate=pl.CostEstimate(flops=0, bytes_accessed=2**20, transcendentals=0),
        name="choose",
    )(spot, plan, keep, given)


def pair_kernel(spot, plan, energy_ref, *refs):
    owns, parts, (row_ref, col_ref) = refs[:8], refs[8:24], refs[24:26]
    outs, own_t, partner, total = refs[26:28], refs[28], refs[29], refs[30]
    s = pl.program_id(0)
    rows, width = owns[0].shape[1:]

    @pl.when(s == 0)
    def _():
        for k in range(CHUNKS):
            for r in range(8):
                own_t[k * width : (k + 1) * width, r * rows : (r + 1) * rows] = owns[4 * k + r % 4][r // 4].T

    for k in range(CHUNKS):
        for r in range(8):
            partner[r * rows : (r + 1) * rows, k * width : (k + 1) * width] = parts[8 * k + r][0]
    coulomb = jnp.dot(own_t[...], partner[...], preferred_element_type=jnp.float32)
    place = spot[2]
    own_energy = energy_ref[(spot[1] * 4 + spot[0]) * 32 + place]
    shift = own_energy + energy_ref[plan[s, place] * 32 + place]
    denominator = shift - row_ref[...] - col_ref[...]
    amplitude = ((2.0 * coulomb - coulomb.T) / denominator).astype(jnp.bfloat16)
    term = lax.dot_general(
        partner[...], amplitude, (((1,), (1,)), ((), ())), preferred_element_type=jnp.float32
    )

    @pl.when(s == 0)
    def _():
        total[...] = term

    @pl.when(s > 0)
    def _():
        total[...] += term

    @pl.when(s == pl.num_programs(0) - 1)
    def _():
        for r in range(8):
            at = slice_of(spot, r // 4, r % 4)
            for t in range(4):
                for k in range(2):
                    first = r * rows + t * 64 + k * 32
                    outs[k][(t % 2) * 16 + 2 * at + t // 2] = total[first : first + 32, :].astype(jnp.bfloat16)


def pair_terms(spot, plan, occupied_energy, owns, parts, virtual_energy):
    _, rows, width = owns[0].shape
    virt = virtual_energy.shape[0]
    steps = plan.shape[0]
    whole = pl.BlockSpec((2, rows, width), lambda s: (0, 0, 0))
    part = pl.BlockSpec((1, rows, width), lambda s: (s, 0, 0))
    out = jax.ShapeDtypeStruct((32, 32, virt), jnp.bfloat16)
    return pl.pallas_call(
        pair_kernel,
        out_shape=[out, out],
        grid=(steps,),
        in_specs=[SMEM, SMEM, SMEM]
        + [whole] * 8
        + [part] * 16
        + [pl.BlockSpec((virt, 1), lambda s: (0, 0)), pl.BlockSpec((1, virt), lambda s: (0, 0))],
        out_specs=[pl.BlockSpec(out.shape, lambda s: (0, 0, 0))] * 2,
        scratch_shapes=[
            pltpu.VMEM((virt, 8 * rows), jnp.bfloat16),
            pltpu.VMEM((8 * rows, virt), jnp.bfloat16),
            pltpu.VMEM((8 * rows, virt), jnp.float32),
        ],
        compiler_params=pltpu.CompilerParams(vmem_limit_bytes=44 * 2**20),
        cost_estimate=pl.CostEstimate(
            flops=steps * 32 * rows * virt * virt,
            bytes_accessed=(steps + 2) * 16 * rows * virt,
            transcendentals=0,
        ),
        name="pair_terms",
    )(spot, plan, occupied_energy, *owns, *parts, virtual_energy[:, None], virtual_energy[None, :])


def body(integrals, metric, occupied_energy, virtual_energy, plan):
    shard, _, virt = integrals.shape
    width = virt // CHUNKS
    y, x, yl, z, c = (lax.axis_index(name) for name, _ in SPLIT)
    spot = jnp.stack([x, c, y * 16 + yl * 8 + z])
    lower = y == 0
    owns, parts = [], []
    for k in range(CHUNKS):
        part = integrals[:, :, k * width : (k + 1) * width]
        halves = [
            lax.dynamic_slice_in_dim(part, 16 * h, 16, 1).transpose(1, 0, 2) for h in (y, 1 - y)
        ]
        here, there = halves[0], shifted(halves[1], "yh", 1)
        turned = jnp.concatenate(
            [jnp.where(lower, here, there), jnp.where(lower, there, here)]
        )
        received = lax.all_to_all(turned, TURNED, 0, 0, tiled=True)
        own = transform(spot, metric, received)
        pieces = [own[0]] + [shifted(own[d], "x", d) for d in (1, 2, 3)]
        keep, give = pick(spot, plan, pieces)
        chosen = choose(spot, plan, keep, shifted(give, "c", 1))
        along = [chosen] + [shifted(chosen, "x", -d) for d in (1, 2, 3)]
        across = [shifted(piece, "c", 1) for piece in along]
        owns += own
        parts += along + across
    density = pair_terms(spot, plan, occupied_energy, owns, parts, virtual_energy)
    outs = []
    for k in range(2):
        gone = lax.all_to_all(density[k], TURNED, 0, 0, tiled=True)
        gone = gone.reshape(2, 16, shard // 2, virt)
        here = lax.dynamic_index_in_dim(gone, y, 0, keepdims=False)
        there = shifted(lax.dynamic_index_in_dim(gone, 1 - y, 0, keepdims=False), "yh", 1)
        both = jnp.concatenate([jnp.where(lower, here, there), jnp.where(lower, there, here)])
        outs.append(both.transpose(1, 0, 2))
    return jnp.concatenate(outs)


def solution(mesh):
    names = tuple(name for name, _ in SPLIT)
    split = Mesh(mesh.devices.reshape(*(size for _, size in SPLIT)), names)
    placed = P(AUX, ("yh", "x"), None)
    return jax.shard_map(
        body, mesh=split, in_specs=(placed, P(), P(), P(), P()), out_specs=placed, check_vma=False
    )
```
